768 devices in a mesh: blk: 16 (over y, x_hi), grp: 48 (over z, x_lo, core).
Axes of the slice: x: 4 (x_hi: 2, x_lo: 2; x = x_hi * 2 + x_lo), y: 8, z: 12, core: 2. Of those that a mesh axis runs over, the one named last changes fastest.
Arguments:
- field: float32 [768, 768, 512], P('grp', 'blk'), may hold values from -7 to 7
- x_panel: float32 [768, 144], P('blk'), as said below
- y_factor: float32 [768, 768], replicated, as said below
- z_factor: float32 [512, 512], replicated, as said below
- scaling: float32 [768, 768, 512], P('grp', 'blk'), may hold values from 0.3 to 3
Outputs:
- updated: float32 [768, 768, 512], P('grp', 'blk')
The draws below stay inside these ranges and needn't reach their ends.
Inputs may be any that keep to these rules, and one draw needn't show every extreme that they name: x_panel[x, j] is zero where j - 48 - (x mod 48) lies outside -48 to 48. y_factor[i, k] is zero where the periodic distance of i and k exceeds 48. z_factor[i, k] is zero where the periodic distance of i and k exceeds 48.
All inputs are finite; a program needn't handle non-finite values.
Results may differ from the reference program's by a relative error of at most 0.0003.
Values sent between devices are 32-bit elements; how exact they have to be, the bound alone decides.
No kernel may reach another device: no remote copies, remote signals or barrier semaphores. Data moves between devices by JAX's collectives and lax.ppermute only.
A program may use at most 32 MiB of HBM per device.

```python
import math
import jax
import jax.numpy as jnp
from jax import lax

HOR = 48
CX = 48
NZ = 512
NX = 768
NY = 768
N_BLK = 16


def band_values(key, dist, horizon):
    rough = jax.random.uniform(key, dist.shape, jnp.float32, 0.5, 1.5)
    distf = dist.astype(jnp.float32)
    sigma = horizon * 1.0
    weight = 0.8 / (1.4936 * sigma) * jnp.exp(-(distf / sigma) ** 2) * rough
    centre = 1.0 + 0.4 * (rough - 1.0)
    values = jnp.where(dist == 0, centre, weight)
    return jnp.where(jnp.abs(dist) <= horizon, values, 0.0).astype(jnp.float32)


def periodic_band(key, count):
    rowid = jnp.arange(count, dtype=jnp.int32)[:, None]
    colid = jnp.arange(count, dtype=jnp.int32)[None, :]
    dist = (colid - rowid + count // 2) % count - count // 2
    return band_values(key, dist, HOR)


def draw_x_panel(key, part):
    rowid = (jnp.arange(NX, dtype=jnp.int32) % CX)[:, None]
    colid = jnp.arange(CX + 2 * HOR, dtype=jnp.int32)[None, :]
    dist = colid - HOR - rowid
    return band_values(key, dist, HOR)


def draw_y_factor(key, part):
    return periodic_band(key, NY)


def draw_z_factor(key, part):
    return periodic_band(key, NZ)


def wavenumbers(key, count, mode_count):
    lowest = max(1, count // (4 * HOR))
    highest = max(lowest + 1, count // HOR + 1)
    magnitude = jax.random.randint(key, (mode_count,), lowest, highest, dtype=jnp.int32)
    signs = 2 * jax.random.randint(jax.random.fold_in(key, 1), (mode_count,), 0, 2, dtype=jnp.int32) - 1
    return magnitude * signs


def draw_field(key, part):
    subkeys = jax.random.split(jax.random.fold_in(key, 11), 6)
    mode_count = 6
    rows_y = jnp.arange(NY, dtype=jnp.int32)[:, None, None]
    rows_x = jnp.arange(NX, dtype=jnp.int32)[None, :, None]
    rows_z = jnp.arange(NZ, dtype=jnp.int32)[None, None, :]
    wave_y = wavenumbers(subkeys[0], NY, mode_count)
    wave_x = wavenumbers(subkeys[1], NX, mode_count)
    wave_z = wavenumbers(subkeys[2], NZ, mode_count)
    amplitude = jax.random.uniform(subkeys[3], (mode_count,), jnp.float32, 0.5, 1.0)
    phases = jax.random.uniform(subkeys[4], (mode_count,), jnp.float32, 0.0, 6.2831853)
    smooth = jnp.zeros((NY, NX, NZ), jnp.float32)
    for mode_index in range(mode_count):
        frac_y = (wave_y[mode_index] * rows_y % NY).astype(jnp.float32) / NY
        frac_x = (wave_x[mode_index] * rows_x % NX).astype(jnp.float32) / NX
        frac_z = (wave_z[mode_index] * rows_z % NZ).astype(jnp.float32) / NZ
        smooth = smooth + amplitude[mode_index] * jnp.cos(6.2831853 * (frac_y + frac_x + frac_z) + phases[mode_index])
    rough_part = jax.random.truncated_normal(subkeys[5], -4.0, 4.0, (NY, NX, NZ), jnp.float32)
    return (rough_part + 0.3 * smooth).astype(jnp.float32)


def shard_levels(rng, dims, shards, least, top_value):
    level = 1.0
    for axis_at, blocks in shards:
        draws = jax.random.uniform(jax.random.fold_in(jax.random.fold_in(rng, 6), axis_at), (blocks,), jnp.float32, least / len(shards), top_value / len(shards))
        level = level * jnp.repeat(jnp.exp(draws), dims[axis_at] // blocks).reshape((-1,) + (1,) * (len(dims) - 1 - axis_at))
    return level


def setup_inputs(seed: int = 0) -> dict:
    streams_of = jax.random.split(jax.random.key(seed), 6)
    field = draw_field(jax.random.fold_in(streams_of[5], 71), 0)
    x_panel = draw_x_panel(jax.random.fold_in(streams_of[5], 71), 0)
    y_factor = draw_y_factor(jax.random.fold_in(streams_of[5], 71), 0)
    z_factor = draw_z_factor(jax.random.fold_in(streams_of[5], 71), 0)
    scaling = jnp.clip(jnp.exp(math.log(3.0) - 2.3025851 * jax.random.uniform(streams_of[4], (NY, NX, NZ), jnp.float32) ** shard_levels(streams_of[4], (NY, NX, NZ), ((0, 48), (1, 16)), -0.2, 0.2)), 0.3, 3.0)
    return dict(field=field, x_panel=x_panel, y_factor=y_factor, z_factor=z_factor, scaling=scaling)


def apply_depth(block, z_factor):
    return lax.dot_general(block, z_factor, (((2,), (1,)), ((), ())), precision=lax.Precision.HIGHEST)


def reference(field, x_panel, y_factor, z_factor, scaling):
    depth = apply_depth(field, z_factor)
    across = jnp.einsum("yk,kxz->yxz", y_factor, depth, precision=lax.Precision.HIGHEST)
    padded = jnp.concatenate([across[:, NX - HOR:], across, across[:, :HOR]], axis=1)

    def one_block(index):
        start = (index * CX).astype(jnp.int32)
        window = lax.dynamic_slice_in_dim(padded, start, CX + 2 * HOR, 1)
        rows = lax.dynamic_slice_in_dim(x_panel, start, CX, 0)
        return jnp.einsum("rj,yjz->yrz", rows, window, precision=lax.Precision.HIGHEST)

    blocks = lax.map(one_block, jnp.arange(N_BLK, dtype=jnp.int32))
    along = jnp.transpose(blocks, (1, 0, 2, 3)).reshape(NY, NX, NZ)
    return along * scaling
```

```python
import functools

import jax
import jax.numpy as jnp
from jax import lax
from jax.experimental import pallas as pl
from jax.experimental.pallas import tpu as pltpu
from jax.sharding import PartitionSpec as P

AXES = ("blk", "grp")
ROWS = 384
EXTRA = 24
INTERPRET = False


def split(v):
    hi = v.astype(jnp.bfloat16)
    return hi, (v - hi.astype(jnp.float32)).astype(jnp.bfloat16)


def dot3(a, b, dims):
    (ah, al), (bh, bl) = a, b
    mul = lambda p, q: lax.dot_general(p, q, (dims, ((), ())), preferred_element_type=jnp.float32)
    return mul(ah, bh) + (mul(ah, bl) + mul(al, bh))


def halves(a, b, low):
    return jnp.where(low, a, pltpu.roll(b, 64, 1)), jnp.where(low, pltpu.roll(a, 64, 1), b)


def low_lanes(rows):
    return lax.broadcasted_iota(jnp.int32, (rows, 128), 1) < 64


def depth_kernel(field_ref, z_ref, extra_ref, out_ref):
    for d in range(8):
        out_ref[d, pl.ds(ROWS, EXTRA), :] = extra_ref[...]
    for u in range(2):
        zs = split(z_ref[pl.ds(256 * u, 256), :])
        for m in range(4):
            ys = (2 * m, 2 * m + 1, 8 + 2 * m, 9 + 2 * m)
            rows = jnp.concatenate([field_ref[pl.ds(48 * y, 48), :] for y in ys], axis=0)
            t = dot3(split(rows), zs, ((1,), (1,)))
            for v in range(2):
                tile = t[:, 128 * v : 128 * v + 128]
                d = 2 * (2 * u + v)
                for i, y in enumerate(ys):
                    part = tile[48 * i : 48 * i + 48]
                    e = jnp.where(low_lanes(24), part[:24], pltpu.roll(part[24:], 64, 1))
                    out_ref[d, pl.ds(y, 24, stride=16), :] = e
                for i in range(2):
                    a = tile[48 * i : 48 * i + 48]
                    b = tile[96 + 48 * i : 144 + 48 * i]
                    o = jnp.where(low_lanes(48), pltpu.roll(a, 64, 1), b)
                    out_ref[d + 1, pl.ds(48 * ys[i], 48), :] = o


def y_pass(own, up, down, ym, emit):
    ys = split(ym[...])
    for xh in range(2):
        def step(i, carry):
            cols = []
            for j in range(2):
                at = pl.ds(pl.multiple_of((2 * i + j) * 16, 16), 16)
                cols.append(
                    jnp.concatenate(
                        [up[3 * xh + s, at, :] for s in range(3)]
                        + [own[4 * xh + s, at, :] for s in range(4)]
                        + [down[3 * xh + s, at, :] for s in range(3)],
                        axis=0,
                    )
                )
            r = dot3(ys, split(jnp.concatenate(cols, axis=1)), ((1,), (0,)))
            for j in range(2):
                emit(xh, 2 * i + j, r[:, 128 * j : 128 * j + 128])
            return carry

        lax.fori_loop(0, 12, step, 0)


def x_pass(own, left, right, xm, emit):
    xs = split(xm[...])
    for s in range(4):
        def step(i, carry):
            cols = []
            for j in range(2):
                at = pl.ds(pl.multiple_of((2 * i + j) * 48, 16), 48)
                cols.append(
                    jnp.concatenate(
                        [left[s, at, :], own[s, at, :], own[4 + s, at, :], right[s, at, :]], axis=0
                    )
                )
            r = dot3(xs, split(jnp.concatenate(cols, axis=1)), ((1,), (0,)))
            for j in range(2):
                emit(s, 2 * i + j, r[:, 128 * j : 128 * j + 128])
            return carry

        lax.fori_loop(0, 4, step, 0)


def first_kernel(core_ref, own, lo, hi, ym, xm, out, plus, minus):
    core = core_ref[0]

    @pl.when(core == 0)
    def _():
        def emit(xh, xx, r):
            for s in range(4):
                w = halves(r[16 * s : 16 * s + 8], r[16 * s + 8 : 16 * s + 16], low_lanes(8))
                for h in range(2):
                    out[4 * xh + s, pl.ds(24 * h + xx, 8, stride=48), :] = w[h]

        y_pass(own, lo, hi, ym, emit)
        for s in range(4):
            plus[s] = out[4 + s]
            minus[s] = out[s]

    @pl.when(core == 1)
    def _():
        def emit(s, yy, r):
            for xh in range(2):
                p = r[48 * xh : 48 * xh + 48]
                q = halves(p[:24], p[24:], low_lanes(24))
                for yh in range(2):
                    out[4 * xh + s, pl.ds(8 * yh + yy, 24, stride=16), :] = q[yh]

        x_pass(own, lo, hi, xm, emit)
        for xh in range(2):
            for s in range(3):
                plus[3 * xh + s] = out[4 * xh + s + 1]
                minus[3 * xh + s] = out[4 * xh + s]


def second_kernel(core_ref, own, lo, hi, ym, xm, out):
    core = core_ref[0]

    @pl.when(core == 0)
    def _():
        def emit(s, yy, r):
            for xh in range(2):
                out[4 * xh + s, pl.ds(pl.multiple_of(48 * yy, 16), 48), :] = r[48 * xh : 48 * xh + 48]

        x_pass(own, lo, hi, xm, emit)

    @pl.when(core == 1)
    def _():
        def emit(xh, xx, r):
            for s in range(4):
                out[4 * xh + s, pl.ds(pl.multiple_of(16 * xx, 16), 16), :] = r[16 * s : 16 * s + 16]

        y_pass(own, lo, hi, ym, emit)


def last_kernel(got, scale_ref, out_ref):
    low = low_lanes(24)
    for t in range(4):
        lanes = pl.ds(128 * t, 128)
        for yy in range(8):
            a = got[2 * t, pl.ds(48 * yy, 48), :]
            for yh in range(2):
                y = 8 * yh + yy
                c = got[2 * t + 1, pl.ds(y, 24, stride=16), :]
                c2 = pltpu.roll(c, 64, 1)
                a2 = pltpu.roll(a, 64, 1) if yh else a
                for h in range(2):
                    at = pl.ds(48 * y + 24 * h, 24)
                    r = jnp.where(low, a2[24 * h : 24 * h + 24], c if h else c2)
                    out_ref[at, lanes] = r * scale_ref[at, lanes]


def call(kernel, shapes, *args, scalar=False):
    specs = [pl.BlockSpec(memory_space=pltpu.VMEM) for _ in args]
    if scalar:
        specs[0] = pl.BlockSpec(memory_space=pltpu.SMEM)
    return pl.pallas_call(
        kernel,
        out_shape=[jax.ShapeDtypeStruct(s, jnp.float32) for s in shapes],
        in_specs=specs,
        out_specs=[pl.BlockSpec(memory_space=pltpu.VMEM) for _ in shapes],
        interpret=INTERPRET,
    )(*args)


def links(mesh):
    n_blk, n_grp = mesh.shape["blk"], mesh.shape["grp"]
    n_y, n_z = n_blk // 2, n_grp // 4

    def place(y, xh, z, r):
        return ((y % n_y) * 2 + xh) * n_grp + (z % n_z) * 4 + r

    everyone = [(y, xh, z, r) for y in range(n_y) for xh in range(2) for z in range(n_z) for r in range(4)]

    def hop(step, along_z):
        pairs = []
        for y, xh, z, r in everyone:
            if r % 2 == along_z:
                to = place(y, xh, z + step, r)
            else:
                to = place(y + step, xh, z, r)
            pairs.append((place(y, xh, z, r), to))
        return pairs

    eights = [[place(y, xh, z, r) for xh in range(2) for r in range(4)] for y in range(n_y) for z in range(n_z)]
    return eights, hop


def on_device(eights, hop, field, x_panel, y_factor, z_factor, scaling):
    grp = lax.axis_index("grp")
    core = grp % 2
    slab, share = grp // 4, grp % 4
    ny = y_factor.shape[0]

    quarter = lax.dynamic_slice_in_dim(x_panel, 12 * share, 12, 0)
    extra = jnp.concatenate([quarter[:, :128], jnp.pad(quarter[:, 128:], ((0, 0), (0, 112)))], axis=0)
    band = lax.dynamic_slice_in_dim(y_factor, 64 * slab, 64, 0)
    band = jnp.concatenate([band[:, ny - 48 :], band, band[:, :64]], axis=1)
    ym = lax.dynamic_slice_in_dim(band, 64 * slab, 160, 1)

    (sent,) = call(depth_kernel, [(8, ROWS + EXTRA, 128)], field.reshape(768, 512), z_factor, extra)
    got = lax.all_to_all(sent, AXES, split_axis=0, concat_axis=0, tiled=True, axis_index_groups=eights)

    tail = got[:, ROWS:, :]
    panel = jnp.concatenate([tail[:, :12], tail[:, 12:, :16]], axis=2).reshape(2, 48, 144)
    xm = jnp.concatenate(
        [jnp.pad(panel[0], ((0, 0), (0, 48))), jnp.pad(panel[1], ((0, 0), (48, 0)))], axis=0
    )
    own = got[:, :ROWS, :]

    def pick(first, second):
        at = jnp.where(core == 0, jnp.array(first), jnp.array(second))
        return jnp.concatenate([lax.dynamic_slice_in_dim(own, at[i], 1, 0) for i in range(6)], axis=0)

    plus = pick((1, 2, 3, 5, 6, 7), (4, 5, 6, 7, 7, 7))
    minus = pick((0, 1, 2, 4, 5, 6), (0, 1, 2, 3, 3, 3))
    lo = lax.ppermute(plus, AXES, hop(1, 0))
    hi = lax.ppermute(minus, AXES, hop(-1, 0))
    flag = core.astype(jnp.int32).reshape(1)
    own, plus, minus = call(
        first_kernel,
        [(8, ROWS, 128), (6, ROWS, 128), (6, ROWS, 128)],
        flag, own, lo, hi, ym, xm, scalar=True,
    )
    lo = lax.ppermute(plus, AXES, hop(1, 1))
    hi = lax.ppermute(minus, AXES, hop(-1, 1))
    (sent,) = call(second_kernel, [(8, ROWS, 128)], flag, own, lo, hi, ym, xm, scalar=True)
    got = lax.all_to_all(sent, AXES, split_axis=0, concat_axis=0, tiled=True, axis_index_groups=eights)
    (out,) = call(last_kernel, [(768, 512)], got, scaling.reshape(768, 512))
    return out.reshape(16, 48, 512)


def solution(mesh):
    eights, hop = links(mesh)
    in_specs = (P("grp", "blk", None), P("blk", None), P(), P(), P("grp", "blk", None))
    return jax.shard_map(
        functools.partial(on_device, eights, hop),
        mesh=mesh,
        in_specs=in_specs,
        out_specs=P("grp", "blk", None),
        check_vma=False,
    )
```

```python
import functools

import jax
import jax.numpy as jnp
from jax import lax
from jax.experimental import pallas as pl
from jax.experimental.pallas import tpu as pltpu
from jax.sharding import PartitionSpec as P

AXES = ("blk", "grp")
ROWS = 384
EXTRA = 24
INTERPRET = False
Y_UNROLL = 2
X_UNROLL = 2
VMEM_LIMIT = 24 * 2**20


def split(v):
    hi = v.astype(jnp.bfloat16)
    return hi, (v - hi.astype(jnp.float32)).astype(jnp.bfloat16)


def dot3(a, b, dims):
    (ah, al), (bh, bl) = a, b
    mul = lambda p, q: lax.dot_general(p, q, (dims, ((), ())), preferred_element_type=jnp.float32)
    return mul(ah, bh) + (mul(ah, bl) + mul(al, bh))


def stack(m):
    return jnp.concatenate(split(m), axis=0)


def factor_dot(m, cols):
    n = m.shape[0] // 2
    ch, cl = split(cols)
    mul = lambda p, q: lax.dot_general(p, q, (((1,), (0,)), ((), ())), preferred_element_type=jnp.float32)
    both = mul(m, ch)
    return both[:n] + (both[n:] + mul(m[:n], cl))


def halves(a, b, low):
    return jnp.where(low, a, pltpu.roll(b, 64, 1)), jnp.where(low, pltpu.roll(a, 64, 1), b)


def core_of():
    return lax.rem(lax.axis_index("grp"), 2)


def low_lanes(rows):
    return lax.broadcasted_iota(jnp.int32, (rows, 128), 1) < 64


def depth_kernel(field_ref, z_ref, panel_ref, out_ref):
    share = lax.rem(lax.axis_index("grp"), 4)
    for s in range(4):
        @pl.when(share == s)
        def _():
            rows = panel_ref[pl.ds(12 * s, 12), :]
            for d in range(8):
                out_ref[d, pl.ds(ROWS, 12), :] = rows[:, :128]
                out_ref[d, pl.ds(ROWS + 12, 12), pl.ds(0, 16)] = rows[:, 128:]

    for u in range(2):
        zs = split(z_ref[pl.ds(256 * u, 256), :])
        for m in range(4):
            ys = (2 * m, 2 * m + 1, 8 + 2 * m, 9 + 2 * m)
            rows = jnp.concatenate([field_ref[pl.ds(48 * y, 48), :] for y in ys], axis=0)
            t = dot3(split(rows), zs, ((1,), (1,)))
            for v in range(2):
                tile = t[:, 128 * v : 128 * v + 128]
                d = 2 * (2 * u + v)
                for i, y in enumerate(ys):
                    part = tile[48 * i : 48 * i + 48]
                    e = jnp.where(low_lanes(24), part[:24], pltpu.roll(part[24:], 64, 1))
                    out_ref[d, pl.ds(y, 24, stride=16), :] = e
                for i in range(2):
                    a = tile[48 * i : 48 * i + 48]
                    b = tile[96 + 48 * i : 144 + 48 * i]
                    o = jnp.where(low_lanes(48), pltpu.roll(a, 64, 1), b)
                    out_ref[d + 1, pl.ds(48 * ys[i], 48), :] = o


def y_pass(own, up, down, ym, emit):
    ys = stack(ym[...])
    for xh in range(2):
        def step(i, carry):
            for k in range(Y_UNROLL):
                cols = []
                for j in range(2):
                    at = pl.ds(pl.multiple_of((2 * (Y_UNROLL * i + k) + j) * 16, 16), 16)
                    cols.append(
                        jnp.concatenate(
                            [up[3 * xh + s, at, :] for s in range(3)]
                            + [own[4 * xh + s, at, :] for s in range(4)]
                            + [down[3 * xh + s, at, :] for s in range(3)],
                            axis=0,
                        )
                    )
                r = factor_dot(ys, jnp.concatenate(cols, axis=1))
                for j in range(2):
                    emit(xh, 2 * (Y_UNROLL * i + k) + j, r[:, 128 * j : 128 * j + 128])
            return carry

        lax.fori_loop(0, 12 // Y_UNROLL, step, 0)


def x_pass(own, left, right, xm, emit):
    xs = stack(xm[...])
    for s in range(4):
        def step(i, carry):
            for k in range(X_UNROLL):
                cols = []
                for j in range(2):
                    at = pl.ds(pl.multiple_of((2 * (X_UNROLL * i + k) + j) * 48, 16), 48)
                    cols.append(
                        jnp.concatenate(
                            [left[s, at, :], own[s, at, :], own[4 + s, at, :], right[s, at, :]], axis=0
                        )
                    )
                r = factor_dot(xs, jnp.concatenate(cols, axis=1))
                for j in range(2):
                    emit(s, 2 * (X_UNROLL * i + k) + j, r[:, 128 * j : 128 * j + 128])
            return carry

        lax.fori_loop(0, 4 // X_UNROLL, step, 0)


def pick_kernel(own, plus, minus):
    core = core_of()

    @pl.when(core == 0)
    def _():
        for i, (p, m) in enumerate(((1, 0), (2, 1), (3, 2), (5, 4), (6, 5), (7, 6))):
            plus[i] = own[p, pl.ds(0, ROWS), :]
            minus[i] = own[m, pl.ds(0, ROWS), :]

    @pl.when(core == 1)
    def _():
        for s in range(4):
            plus[s] = own[4 + s, pl.ds(0, ROWS), :]
            minus[s] = own[s, pl.ds(0, ROWS), :]


def first_kernel(own, lo, hi, ym, xm, out, plus, minus):
    core = core_of()

    @pl.when(core == 0)
    def _():
        def emit(xh, xx, r):
            for s in range(4):
                w = halves(r[16 * s : 16 * s + 8], r[16 * s + 8 : 16 * s + 16], low_lanes(8))
                for h in range(2):
                    out[4 * xh + s, pl.ds(24 * h + xx, 8, stride=48), :] = w[h]

        y_pass(own, lo, hi, ym, emit)
        for s in range(4):
            plus[s] = out[4 + s]
            minus[s] = out[s]

    @pl.when(core == 1)
    def _():
        def emit(s, yy, r):
            for xh in range(2):
                p = r[48 * xh : 48 * xh + 48]
                q = halves(p[:24], p[24:], low_lanes(24))
                for yh in range(2):
                    out[4 * xh + s, pl.ds(8 * yh + yy, 24, stride=16), :] = q[yh]

        x_pass(own, lo, hi, xm, emit)
        for xh in range(2):
            for s in range(3):
                plus[3 * xh + s] = out[4 * xh + s + 1]
                minus[3 * xh + s] = out[4 * xh + s]


def second_kernel(own, lo, hi, ym, xm, out):
    core = core_of()

    @pl.when(core == 0)
    def _():
        def emit(s, yy, r):
            for xh in range(2):
                out[4 * xh + s, pl.ds(pl.multiple_of(48 * yy, 16), 48), :] = r[48 * xh : 48 * xh + 48]

        x_pass(own, lo, hi, xm, emit)

    @pl.when(core == 1)
    def _():
        def emit(xh, xx, r):
            for s in range(4):
                out[4 * xh + s, pl.ds(pl.multiple_of(16 * xx, 16), 16), :] = r[16 * s : 16 * s + 16]

        y_pass(own, lo, hi, ym, emit)


def last_kernel(got, scale_ref, out_ref):
    low = low_lanes(24)
    for t in range(4):
        lanes = pl.ds(128 * t, 128)
        for yy in range(8):
            a = got[2 * t, pl.ds(48 * yy, 48), :]
            for yh in range(2):
                y = 8 * yh + yy
                c = got[2 * t + 1, pl.ds(y, 24, stride=16), :]
                c2 = pltpu.roll(c, 64, 1)
                a2 = pltpu.roll(a, 64, 1) if yh else a
                for h in range(2):
                    at = pl.ds(48 * y + 24 * h, 24)
                    r = jnp.where(low, a2[24 * h : 24 * h + 24], c if h else c2)
                    out_ref[at, lanes] = r * scale_ref[at, lanes]


def call(kernel, shapes, *args, plain=False):
    specs = [pl.BlockSpec(memory_space=pltpu.VMEM) for _ in args]
    outs = [jax.ShapeDtypeStruct(s, jnp.float32) for s in shapes]
    if not INTERPRET:
        args = [pltpu.with_memory_space_constraint(a, pltpu.VMEM) for a in args]
        if not plain:
            outs = [pltpu.VMEM(s, jnp.float32) for s in shapes]
    return pl.pallas_call(
        kernel,
        out_shape=outs,
        in_specs=specs,
        out_specs=[pl.BlockSpec(memory_space=pltpu.VMEM) for _ in shapes],
        compiler_params=pltpu.CompilerParams(vmem_limit_bytes=VMEM_LIMIT),
        interpret=INTERPRET,
    )(*args)


def links(mesh):
    n_blk, n_grp = mesh.shape["blk"], mesh.shape["grp"]
    n_y, n_z = n_blk // 2, n_grp // 4

    def place(y, xh, z, r):
        return ((y % n_y) * 2 + xh) * n_grp + (z % n_z) * 4 + r

    everyone = [(y, xh, z, r) for y in range(n_y) for xh in range(2) for z in range(n_z) for r in range(4)]

    def hop(step, along_z):
        pairs = []
        for y, xh, z, r in everyone:
            if r % 2 == along_z:
                to = place(y, xh, z + step, r)
            else:
                to = place(y + step, xh, z, r)
            pairs.append((place(y, xh, z, r), to))
        return pairs

    eights = [[place(y, xh, z, r) for xh in range(2) for r in range(4)] for y in range(n_y) for z in range(n_z)]
    return eights, hop


def on_device(eights, hop, field, x_panel, y_factor, z_factor, scaling):
    grp = lax.axis_index("grp")
    slab = grp // 4
    ny = y_factor.shape[0]

    band = lax.dynamic_slice_in_dim(y_factor, 64 * slab, 64, 0)
    band = jnp.concatenate([band[:, ny - 48 :], band, band[:, :64]], axis=1)
    ym = lax.dynamic_slice_in_dim(band, 64 * slab, 160, 1)

    (sent,) = call(depth_kernel, [(8, ROWS + EXTRA, 128)], field.reshape(768, 512), z_factor, x_panel, plain=True)
    got = lax.all_to_all(sent, AXES, split_axis=0, concat_axis=0, tiled=True, axis_index_groups=eights)

    tail = got[:, ROWS:, :]
    panel = jnp.concatenate([tail[:, :12], tail[:, 12:, :16]], axis=2).reshape(2, 48, 144)
    xm = jnp.concatenate(
        [jnp.pad(panel[0], ((0, 0), (0, 48))), jnp.pad(panel[1], ((0, 0), (48, 0)))], axis=0
    )
    plus, minus = call(pick_kernel, [(6, ROWS, 128), (6, ROWS, 128)], got)
    lo = lax.ppermute(plus, AXES, hop(1, 0))
    hi = lax.ppermute(minus, AXES, hop(-1, 0))
    own, plus, minus = call(
        first_kernel,
        [(8, ROWS, 128), (6, ROWS, 128), (6, ROWS, 128)],
        got, lo, hi, ym, xm,
    )
    lo = lax.ppermute(plus, AXES, hop(1, 1))
    hi = lax.ppermute(minus, AXES, hop(-1, 1))
    (sent,) = call(second_kernel, [(8, ROWS, 128)], own, lo, hi, ym, xm)
    got = lax.all_to_all(sent, AXES, split_axis=0, concat_axis=0, tiled=True, axis_index_groups=eights)
    (out,) = call(last_kernel, [(768, 512)], got, scaling.reshape(768, 512), plain=True)
    return out.reshape(16, 48, 512)


def solution(mesh):
    eights, hop = links(mesh)
    in_specs = (P("grp", "blk", None), P("blk", None), P(), P(), P("grp", "blk", None))
    return jax.shard_map(
        functools.partial(on_device, eights, hop),
        mesh=mesh,
        in_specs=in_specs,
        out_specs=P("grp", "blk", None),
        check_vma=False,
    )
```

```python
import functools

import jax
import jax.numpy as jnp
from jax import lax
from jax.experimental import pallas as pl
from jax.experimental.pallas import tpu as pltpu
from jax.sharding import PartitionSpec as P

AXES = ("blk", "grp")
ROWS = 384
EXTRA = 24
INTERPRET = False
Y_UNROLL = 2
X_UNROLL = 2
VMEM_LIMIT = 24 * 2**20


def split(v):
    hi = v.astype(jnp.bfloat16)
    return hi, (v - hi.astype(jnp.float32)).astype(jnp.bfloat16)


def dot3(a, b, dims):
    (ah, al), (bh, bl) = a, b
    mul = lambda p, q: lax.dot_general(p, q, (dims, ((), ())), preferred_element_type=jnp.float32)
    return mul(ah, bh) + (mul(ah, bl) + mul(al, bh))


def stack(m):
    return jnp.concatenate(split(m), axis=0)


def factor_dot(m, cols):
    n = m.shape[0] // 2
    ch, cl = split(cols)
    mul = lambda p, q: lax.dot_general(p, q, (((1,), (0,)), ((), ())), preferred_element_type=jnp.float32)
    both = mul(m, ch)
    return both[:n] + (both[n:] + mul(m[:n], cl))


def halves(a, b, low):
    return jnp.where(low, a, pltpu.roll(b, 64, 1)), jnp.where(low, pltpu.roll(a, 64, 1), b)


def core_of():
    return lax.rem(lax.axis_index("grp"), 2)


def low_lanes(rows):
    return lax.broadcasted_iota(jnp.int32, (rows, 128), 1) < 64


def depth_kernel(field_hbm, z_hbm, panel_hbm, out_ref, field_ref, z_ref, panel_ref, sems):
    panel_copy = pltpu.make_async_copy(panel_hbm, panel_ref, sems.at[10])
    field_copies, z_copies = [], []
    for u in range(2):
        at = pl.ds(256 * u, 256)
        z_copies.append(pltpu.make_async_copy(z_hbm.at[at, :], z_ref.at[at, :], sems.at[8 + u]))
    for m in range(4):
        for i in range(2):
            at = pl.ds(48 * (8 * i + 2 * m), 96)
            field_copies.append(pltpu.make_async_copy(field_hbm.at[at, :], field_ref.at[at, :], sems.at[2 * m + i]))
    for c in [z_copies[0]] + field_copies + [z_copies[1], panel_copy]:
        c.start()

    for u in range(2):
        z_copies[u].wait()
        zs = split(z_ref[pl.ds(256 * u, 256), :])
        for m in range(4):
            if u == 0 and m % 2 == 0:
                for c in field_copies[2 * m : 2 * m + 4]:
                    c.wait()
            ys = (2 * m, 2 * m + 1, 8 + 2 * m, 9 + 2 * m)
            rows = jnp.concatenate([field_ref[pl.ds(96 * m, 96), :], field_ref[pl.ds(384 + 96 * m, 96), :]], axis=0)
            t = dot3(split(rows), zs, ((1,), (1,)))
            for v in range(2):
                tile = t[:, 128 * v : 128 * v + 128]
                d = 2 * (2 * u + v)
                for i, y in enumerate(ys):
                    part = tile[48 * i : 48 * i + 48]
                    e = jnp.where(low_lanes(24), part[:24], pltpu.roll(part[24:], 64, 1))
                    out_ref[d, pl.ds(y, 24, stride=16), :] = e
                for i in range(2):
                    a = tile[48 * i : 48 * i + 48]
                    b = tile[96 + 48 * i : 144 + 48 * i]
                    o = jnp.where(low_lanes(48), pltpu.roll(a, 64, 1), b)
                    out_ref[d + 1, pl.ds(48 * ys[i], 48), :] = o

    panel_copy.wait()
    share = lax.rem(lax.axis_index("grp"), 4)
    for s in range(4):
        @pl.when(share == s)
        def _():
            rows = panel_ref[pl.ds(12 * s, 12), :]
            for d in range(8):
                out_ref[d, pl.ds(ROWS, 12), :] = rows[:, :128]
                out_ref[d, pl.ds(ROWS + 12, 12), pl.ds(0, 16)] = rows[:, 128:]


def y_pass(own, up, down, ym, emit):
    ys = stack(ym[:, :160])
    for xh in range(2):
        def step(i, carry):
            for k in range(Y_UNROLL):
                cols = []
                for j in range(2):
                    at = pl.ds(pl.multiple_of((2 * (Y_UNROLL * i + k) + j) * 16, 16), 16)
                    cols.append(
                        jnp.concatenate(
                            [up[3 * xh + s, at, :] for s in range(3)]
                            + [own[4 * xh + s, at, :] for s in range(4)]
                            + [down[3 * xh + s, at, :] for s in range(3)],
                            axis=0,
                        )
                    )
                r = factor_dot(ys, jnp.concatenate(cols, axis=1))
                for j in range(2):
                    emit(xh, 2 * (Y_UNROLL * i + k) + j, r[:, 128 * j : 128 * j + 128])
            return carry

        lax.fori_loop(0, 12 // Y_UNROLL, step, 0)


def x_pass(own, left, right, xm, emit):
    xs = stack(xm[:, :192])
    for s in range(4):
        def step(i, carry):
            for k in range(X_UNROLL):
                cols = []
                for j in range(2):
                    at = pl.ds(pl.multiple_of((2 * (X_UNROLL * i + k) + j) * 48, 16), 48)
                    cols.append(
                        jnp.concatenate(
                            [left[s, at, :], own[s, at, :], own[4 + s, at, :], right[s, at, :]], axis=0
                        )
                    )
                r = factor_dot(xs, jnp.concatenate(cols, axis=1))
                for j in range(2):
                    emit(s, 2 * (X_UNROLL * i + k) + j, r[:, 128 * j : 128 * j + 128])
            return carry

        lax.fori_loop(0, 4 // X_UNROLL, step, 0)


def pick_kernel(own, y_ref, plus, minus, ym, xm):
    core = core_of()
    slab = lax.div(lax.axis_index("grp"), 4)
    ny = y_ref.shape[0]
    @pl.when(core == 0)
    def _():
        for i, (p, m) in enumerate(((1, 0), (2, 1), (3, 2), (5, 4), (6, 5), (7, 6))):
            plus[i] = own[p, pl.ds(0, ROWS), :]
            minus[i] = own[m, pl.ds(0, ROWS), :]

    @pl.when(core == 1)
    def _():
        for s in range(4):
            plus[s] = own[4 + s, pl.ds(0, ROWS), :]
            minus[s] = own[s, pl.ds(0, ROWS), :]

    few = lax.broadcasted_iota(jnp.int32, (12, 128), 1) < 16
    for xh in range(2):
        for s in range(4):
            p = own[4 * xh + s, pl.ds(ROWS, 12), :]
            q = jnp.where(few, own[4 * xh + s, pl.ds(ROWS + 12, 12), :], 0.0)
            w = jnp.concatenate([p, q], axis=1)
            xm[pl.ds(48 * xh + 12 * s, 12), :] = pltpu.roll(w, 48, 1) if xh else w
    shift = lax.rem(ny + 48 - 64 * slab, ny)
    ym[...] = pltpu.roll(y_ref[pl.ds(pl.multiple_of(64 * slab, 64), 64), :], shift, 1)[:, :256]


def first_kernel(own, lo, hi, ym, xm, out, plus, minus):
    core = core_of()

    @pl.when(core == 0)
    def _():
        def emit(xh, xx, r):
            for s in range(4):
                w = halves(r[16 * s : 16 * s + 8], r[16 * s + 8 : 16 * s + 16], low_lanes(8))
                for h in range(2):
                    out[4 * xh + s, pl.ds(24 * h + xx, 8, stride=48), :] = w[h]

        y_pass(own, lo, hi, ym, emit)
        for s in range(4):
            plus[s] = out[4 + s]
            minus[s] = out[s]

    @pl.when(core == 1)
    def _():
        def emit(s, yy, r):
            for xh in range(2):
                p = r[48 * xh : 48 * xh + 48]
                q = halves(p[:24], p[24:], low_lanes(24))
                for yh in range(2):
                    out[4 * xh + s, pl.ds(8 * yh + yy, 24, stride=16), :] = q[yh]

        x_pass(own, lo, hi, xm, emit)
        for xh in range(2):
            for s in range(3):
                plus[3 * xh + s] = out[4 * xh + s + 1]
                minus[3 * xh + s] = out[4 * xh + s]


def second_kernel(own, lo, hi, ym, xm, out):
    core = core_of()

    @pl.when(core == 0)
    def _():
        def emit(s, yy, r):
            for xh in range(2):
                out[4 * xh + s, pl.ds(pl.multiple_of(48 * yy, 16), 48), :] = r[48 * xh : 48 * xh + 48]

        x_pass(own, lo, hi, xm, emit)

    @pl.when(core == 1)
    def _():
        def emit(xh, xx, r):
            for s in range(4):
                out[4 * xh + s, pl.ds(pl.multiple_of(16 * xx, 16), 16), :] = r[16 * s : 16 * s + 16]

        y_pass(own, lo, hi, ym, emit)


def last_kernel(got, scale_ref, out_ref):
    low = low_lanes(24)
    for t in range(4):
        lanes = pl.ds(128 * t, 128)
        for yy in range(8):
            a = got[2 * t, pl.ds(48 * yy, 48), :]
            for yh in range(2):
                y = 8 * yh + yy
                c = got[2 * t + 1, pl.ds(y, 24, stride=16), :]
                c2 = pltpu.roll(c, 64, 1)
                a2 = pltpu.roll(a, 64, 1) if yh else a
                for h in range(2):
                    at = pl.ds(48 * y + 24 * h, 24)
                    r = jnp.where(low, a2[24 * h : 24 * h + 24], c if h else c2)
                    out_ref[at, lanes] = r * scale_ref[at, lanes]


def call(kernel, shapes, *args, hbm=(), plain=False, scratch=()):
    vmem = pl.BlockSpec(memory_space=pltpu.VMEM)
    outs = [jax.ShapeDtypeStruct(s, jnp.float32) for s in shapes]
    if not INTERPRET:
        args = [pltpu.with_memory_space_constraint(a, pltpu.HBM if i in hbm else pltpu.VMEM) for i, a in enumerate(args)]
        if not plain:
            outs = [pltpu.VMEM(s, jnp.float32) for s in shapes]
    return pl.pallas_call(
        kernel,
        out_shape=outs,
        in_specs=[pl.BlockSpec(memory_space=pltpu.HBM) if i in hbm else vmem for i in range(len(args))],
        out_specs=[vmem for _ in shapes],
        scratch_shapes=list(scratch),
        compiler_params=pltpu.CompilerParams(vmem_limit_bytes=VMEM_LIMIT),
        interpret=INTERPRET,
    )(*args)


def links(mesh):
    n_blk, n_grp = mesh.shape["blk"], mesh.shape["grp"]
    n_y, n_z = n_blk // 2, n_grp // 4

    def place(y, xh, z, r):
        return ((y % n_y) * 2 + xh) * n_grp + (z % n_z) * 4 + r

    everyone = [(y, xh, z, r) for y in range(n_y) for xh in range(2) for z in range(n_z) for r in range(4)]

    def hop(step, along_z):
        pairs = []
        for y, xh, z, r in everyone:
            if r % 2 == along_z:
                to = place(y, xh, z + step, r)
            else:
                to = place(y + step, xh, z, r)
            pairs.append((place(y, xh, z, r), to))
        return pairs

    eights = [[place(y, xh, z, r) for xh in range(2) for r in range(4)] for y in range(n_y) for z in range(n_z)]
    return eights, hop


def on_device(eights, hop, field, x_panel, y_factor, z_factor, scaling):
    (sent,) = call(
        depth_kernel, [(8, ROWS + EXTRA, 128)], field.reshape(768, 512), z_factor, x_panel,
        hbm=(0, 1, 2),
        scratch=[
            pltpu.VMEM((768, 512), jnp.float32),
            pltpu.VMEM((512, 512), jnp.float32),
            pltpu.VMEM((48, 144), jnp.float32),
            pltpu.SemaphoreType.DMA((11,)),
        ],
    )
    got = lax.all_to_all(sent, AXES, split_axis=0, concat_axis=0, tiled=True, axis_index_groups=eights)

    plus, minus, ym, xm = call(
        pick_kernel, [(6, ROWS, 128), (6, ROWS, 128), (64, 256), (96, 256)], got, y_factor,
    )
    lo = lax.ppermute(plus, AXES, hop(1, 0))
    hi = lax.ppermute(minus, AXES, hop(-1, 0))
    own, plus, minus = call(
        first_kernel,
        [(8, ROWS, 128), (6, ROWS, 128), (6, ROWS, 128)],
        got, lo, hi, ym, xm,
    )
    lo = lax.ppermute(plus, AXES, hop(1, 1))
    hi = lax.ppermute(minus, AXES, hop(-1, 1))
    (sent,) = call(second_kernel, [(8, ROWS, 128)], own, lo, hi, ym, xm)
    got = lax.all_to_all(sent, AXES, split_axis=0, concat_axis=0, tiled=True, axis_index_groups=eights)
    (out,) = call(last_kernel, [(768, 512)], got, scaling.reshape(768, 512), plain=True)
    return out.reshape(16, 48, 512)


def solution(mesh):
    eights, hop = links(mesh)
    in_specs = (P("grp", "blk", None), P("blk", None), P(), P(), P("grp", "blk", None))
    return jax.shard_map(
        functools.partial(on_device, eights, hop),
        mesh=mesh,
        in_specs=in_specs,
        out_specs=P("grp", "blk", None),
        check_vma=False,
    )
```

```python
import functools

import jax
import jax.numpy as jnp
from jax import lax
from jax.experimental import pallas as pl
from jax.experimental.pallas import tpu as pltpu
from jax.sharding import PartitionSpec as P

AXES = ("blk", "grp")
ROWS = 384
EXTRA = 24
INTERPRET = False
Y_UNROLL = 2
X_UNROLL = 4
Z_PAIRS = 2
Z_WAIT = 4
VMEM_LIMIT = 24 * 2**20


def split(v):
    hi = v.astype(jnp.bfloat16)
    return hi, (v - hi.astype(jnp.float32)).astype(jnp.bfloat16)


def dot3(a, b, dims):
    (ah, al), (bh, bl) = a, b
    mul = lambda p, q: lax.dot_general(p, q, (dims, ((), ())), preferred_element_type=jnp.float32)
    return mul(ah, bh) + (mul(ah, bl) + mul(al, bh))


def stack(m):
    return jnp.concatenate(split(m), axis=0)


def factor_dot(m, cols):
    n = m.shape[0] // 2
    ch, cl = split(cols)
    mul = lambda p, q: lax.dot_general(p, q, (((1,), (0,)), ((), ())), preferred_element_type=jnp.float32)
    both = mul(m, ch)
    return both[:n] + (both[n:] + mul(m[:n], cl))


def halves(a, b, low):
    return jnp.where(low, a, pltpu.roll(b, 64, 1)), jnp.where(low, pltpu.roll(a, 64, 1), b)


def core_of():
    return lax.rem(lax.axis_index("grp"), 2)


def low_lanes(rows):
    return lax.broadcasted_iota(jnp.int32, (rows, 128), 1) < 64


class Pair:
    def __init__(self, *copies):
        self.copies = copies

    def start(self):
        for c in self.copies:
            c.start()

    def wait(self):
        for c in self.copies:
            c.wait()


def beside(rows, t, low):
    tile = lambda k: rows[:, 128 * (k % 4) : 128 * (k % 4) + 128]
    return jnp.concatenate([tile(t), jnp.where(low, tile(t + 1), tile(t - 1))], axis=1)


def depth_kernel(field_hbm, z_hbm, panel_hbm, out_ref, field_ref, z_ref, w_ref, panel_ref, sems):
    panel_copy = pltpu.make_async_copy(panel_hbm, panel_ref, sems.at[18])
    field_copies, z_copies = [], []
    for u in range(2):
        at = pl.ds(256 * u, 256)
        z_copies.append(pltpu.make_async_copy(z_hbm.at[at, :], z_ref.at[at, :], sems.at[16 + u]))
    for y in range(8):
        for i in range(2):
            at = pl.ds(48 * (8 * i + y), 48)
            field_copies.append(pltpu.make_async_copy(field_hbm.at[at, :], field_ref.at[at, :], sems.at[2 * y + i]))
    field_copies = [Pair(*field_copies[2 * y : 2 * y + 2]) for y in range(8)]
    for c in z_copies + field_copies + [panel_copy]:
        c.start()

    for c in z_copies:
        c.wait()
    for t in range(4):
        both = split(beside(z_ref[pl.ds(128 * t, 128), :], t, low_lanes(128)))
        w_ref[t] = jnp.concatenate(both, axis=0)
    low = low_lanes(48)
    for m in range(8 // Z_PAIRS):
        ys = [Z_PAIRS * m + i for i in range(Z_PAIRS)]
        if (Z_PAIRS * m) % Z_WAIT == 0:
            for c in field_copies[Z_PAIRS * m : Z_PAIRS * m + Z_WAIT]:
                c.wait()
        ys = ys + [8 + y for y in ys]
        n = 48 * len(ys)
        rows = jnp.concatenate([field_ref[pl.ds(48 * y, 48), :] for y in ys], axis=0)
        for t in range(4):
            r = lax.dot_general(
                jnp.concatenate(split(beside(rows, t, low_lanes(n))), axis=0), w_ref[t],
                (((1,), (1,)), ((), ())), preferred_element_type=jnp.float32,
            )
            tile = r[:n, :128] + (r[:n, 128:] + r[n:, :128])
            d = 2 * t
            for i, y in enumerate(ys):
                part = tile[48 * i : 48 * i + 48]
                e = jnp.where(low_lanes(24), part[:24], pltpu.roll(part[24:], 64, 1))
                out_ref[d, pl.ds(y, 24, stride=16), :] = e
            for i in range(Z_PAIRS):
                a = tile[48 * i : 48 * i + 48]
                b = tile[48 * (Z_PAIRS + i) : 48 * (Z_PAIRS + i) + 48]
                out_ref[d + 1, pl.ds(48 * ys[i], 48), :] = jnp.where(low, pltpu.roll(a, 64, 1), b)

    panel_copy.wait()
    share = lax.rem(lax.axis_index("grp"), 4)
    for s in range(4):
        @pl.when(share == s)
        def _():
            rows = panel_ref[pl.ds(12 * s, 12), :]
            for d in range(8):
                out_ref[d, pl.ds(ROWS, 12), :] = rows[:, :128]
                out_ref[d, pl.ds(ROWS + 12, 12), pl.ds(0, 16)] = rows[:, 128:]


def loop(count, unroll, body):
    def step(i, carry):
        for k in range(unroll):
            body(unroll * i + k)
        return carry

    lax.fori_loop(0, count // unroll, step, 0)


def pair_of(body):
    return [body(0), body(1)]


def y_rows(x):
    return pl.ds(pl.multiple_of(16 * x, 16), 16)


def x_rows(y):
    return pl.ds(pl.multiple_of(48 * y, 16), 48)


def keep(part, at, n, r):
    for j in range(2):
        part[pl.ds(pl.multiple_of(n * (at + j), 32), n), :] = r[:, 128 * j : 128 * j + 128]


def part_rows(part, at, n):
    return part[pl.ds(pl.multiple_of(n * at, 32), n), :]


def lower_kernel(y_core, own, lo, ym, xm, part):
    core = core_of()

    @pl.when(core == y_core)
    def _():
        ys = stack(ym[:, :112])
        for xh in range(2):
            def body(i):
                def column(j):
                    at = y_rows(2 * i + j)
                    return jnp.concatenate(
                        [lo[3 * xh + s, at, :] for s in range(3)] + [own[4 * xh + s, at, :] for s in range(4)], axis=0
                    )

                keep(part, 24 * xh + 2 * i, 64, factor_dot(ys, jnp.concatenate(pair_of(column), axis=1)))

            loop(12, Y_UNROLL, body)

    @pl.when(core != y_core)
    def _():
        xs = stack(xm[:, :144])
        for s in range(4):
            def body(i):
                def column(j):
                    at = x_rows(2 * i + j)
                    return jnp.concatenate([lo[s, at, :], own[s, at, :], own[4 + s, at, :]], axis=0)

                keep(part, 8 * s + 2 * i, 96, factor_dot(xs, jnp.concatenate(pair_of(column), axis=1)))

            loop(4, X_UNROLL, body)


def y_finish(part, hi, ym, emit):
    ys = stack(ym[:, 128:176])
    for xh in range(2):
        def body(i):
            def column(j):
                return jnp.concatenate([hi[3 * xh + s, y_rows(2 * i + j), :] for s in range(3)], axis=0)

            r = factor_dot(ys, jnp.concatenate(pair_of(column), axis=1))
            for j in range(2):
                x = 2 * i + j
                emit(xh, x, part_rows(part, 24 * xh + x, 64) + r[:, 128 * j : 128 * j + 128])

        loop(12, Y_UNROLL, body)


def x_finish(part, hi, xu, emit):
    xs = stack(xu[:, :48])
    for s in range(4):
        def body(i):
            r = factor_dot(xs, jnp.concatenate(pair_of(lambda j: hi[s, x_rows(2 * i + j), :]), axis=1))
            for j in range(2):
                y = 2 * i + j
                p = part_rows(part, 8 * s + y, 96)
                emit(s, y, (p[:48], p[48:] + r[:, 128 * j : 128 * j + 128]))

        loop(4, X_UNROLL, body)


def pick_kernel(own, y_ref, plus, minus, ym, xm, xu):
    core = core_of()
    slab = lax.div(lax.axis_index("grp"), 4)
    ny = y_ref.shape[0]
    @pl.when(core == 0)
    def _():
        for i, (p, m) in enumerate(((1, 0), (2, 1), (3, 2), (5, 4), (6, 5), (7, 6))):
            plus[i] = own[p, pl.ds(0, ROWS), :]
            minus[i] = own[m, pl.ds(0, ROWS), :]

    @pl.when(core == 1)
    def _():
        for s in range(4):
            plus[s] = own[4 + s, pl.ds(0, ROWS), :]
            minus[s] = own[s, pl.ds(0, ROWS), :]

    few = lax.broadcasted_iota(jnp.int32, (12, 128), 1) < 16
    for xh in range(2):
        for s in range(4):
            p = own[4 * xh + s, pl.ds(ROWS, 12), :]
            q = jnp.where(few, own[4 * xh + s, pl.ds(ROWS + 12, 12), :], 0.0)
            w = jnp.concatenate([p, q], axis=1)
            xm[pl.ds(48 * xh + 12 * s, 12), :] = pltpu.roll(w, 48, 1) if xh else w
            if xh:
                xu[pl.ds(12 * s, 12), :] = pltpu.roll(w, 160, 1)[:, :128]
    rows = y_ref[pl.ds(pl.multiple_of(64 * slab, 64), 64), :]
    for i, first in enumerate((-48, 64)):
        shift = lax.rem(2 * ny - first - 64 * slab, ny)
        ym[:, pl.ds(128 * i, 128)] = pltpu.roll(rows, shift, 1)[:, :128]


def first_kernel(part, hi, ym, xu, out, plus, minus):
    core = core_of()

    @pl.when(core == 0)
    def _():
        def emit(xh, xx, r):
            for s in range(4):
                w = halves(r[16 * s : 16 * s + 8], r[16 * s + 8 : 16 * s + 16], low_lanes(8))
                for h in range(2):
                    out[4 * xh + s, pl.ds(24 * h + xx, 8, stride=48), :] = w[h]

        y_finish(part, hi, ym, emit)
        for s in range(4):
            plus[s] = out[4 + s]
            minus[s] = out[s]

    @pl.when(core == 1)
    def _():
        def emit(s, yy, r):
            for xh in range(2):
                q = halves(r[xh][:24], r[xh][24:], low_lanes(24))
                for yh in range(2):
                    out[4 * xh + s, pl.ds(8 * yh + yy, 24, stride=16), :] = q[yh]

        x_finish(part, hi, xu, emit)
        for xh in range(2):
            for s in range(3):
                plus[3 * xh + s] = out[4 * xh + s + 1]
                minus[3 * xh + s] = out[4 * xh + s]


def second_kernel(part, hi, ym, xu, out):
    core = core_of()

    @pl.when(core == 0)
    def _():
        def emit(s, yy, r):
            for xh in range(2):
                out[4 * xh + s, x_rows(yy), :] = r[xh]

        x_finish(part, hi, xu, emit)

    @pl.when(core == 1)
    def _():
        def emit(xh, xx, r):
            for s in range(4):
                out[4 * xh + s, y_rows(xx), :] = r[16 * s : 16 * s + 16]

        y_finish(part, hi, ym, emit)


def last_kernel(got, scale_ref, out_ref):
    low = low_lanes(24)
    for t in range(4):
        lanes = pl.ds(128 * t, 128)
        for yy in range(8):
            a = got[2 * t, pl.ds(48 * yy, 48), :]
            for yh in range(2):
                y = 8 * yh + yy
                c = got[2 * t + 1, pl.ds(y, 24, stride=16), :]
                c2 = pltpu.roll(c, 64, 1)
                a2 = pltpu.roll(a, 64, 1) if yh else a
                for h in range(2):
                    at = pl.ds(48 * y + 24 * h, 24)
                    r = jnp.where(low, a2[24 * h : 24 * h + 24], c if h else c2)
                    out_ref[at, lanes] = r * scale_ref[at, lanes]


def call(kernel, shapes, *args, hbm=(), plain=False, scratch=()):
    vmem = pl.BlockSpec(memory_space=pltpu.VMEM)
    outs = [jax.ShapeDtypeStruct(s, jnp.float32) for s in shapes]
    if not INTERPRET:
        args = [pltpu.with_memory_space_constraint(a, pltpu.HBM if i in hbm else pltpu.VMEM) for i, a in enumerate(args)]
        if not plain:
            outs = [pltpu.VMEM(s, jnp.float32) for s in shapes]
    return pl.pallas_call(
        kernel,
        out_shape=outs,
        in_specs=[pl.BlockSpec(memory_space=pltpu.HBM) if i in hbm else vmem for i in range(len(args))],
        out_specs=[vmem for _ in shapes],
        scratch_shapes=list(scratch),
        compiler_params=pltpu.CompilerParams(vmem_limit_bytes=VMEM_LIMIT),
        interpret=INTERPRET,
    )(*args)


def links(mesh):
    n_blk, n_grp = mesh.shape["blk"], mesh.shape["grp"]
    n_y, n_z = n_blk // 2, n_grp // 4

    def place(y, xh, z, r):
        return ((y % n_y) * 2 + xh) * n_grp + (z % n_z) * 4 + r

    everyone = [(y, xh, z, r) for y in range(n_y) for xh in range(2) for z in range(n_z) for r in range(4)]

    def hop(step, along_z):
        pairs = []
        for y, xh, z, r in everyone:
            if r % 2 == along_z:
                to = place(y, xh, z + step, r)
            else:
                to = place(y + step, xh, z, r)
            pairs.append((place(y, xh, z, r), to))
        return pairs

    eights = [[place(y, xh, z, r) for xh in range(2) for r in range(4)] for y in range(n_y) for z in range(n_z)]
    return eights, hop


def on_device(eights, hop, field, x_panel, y_factor, z_factor, scaling):
    (sent,) = call(
        depth_kernel, [(8, ROWS + EXTRA, 128)], field.reshape(768, 512), z_factor, x_panel,
        hbm=(0, 1, 2),
        scratch=[
            pltpu.VMEM((768, 512), jnp.float32),
            pltpu.VMEM((512, 512), jnp.float32),
            pltpu.VMEM((4, 256, 256), jnp.bfloat16),
            pltpu.VMEM((48, 144), jnp.float32),
            pltpu.SemaphoreType.DMA((19,)),
        ],
    )
    got = lax.all_to_all(sent, AXES, split_axis=0, concat_axis=0, tiled=True, axis_index_groups=eights)

    plus, minus, ym, xm, xu = call(
        pick_kernel, [(6, ROWS, 128), (6, ROWS, 128), (64, 256), (96, 256), (48, 128)], got, y_factor
    )
    lo = lax.ppermute(plus, AXES, hop(1, 0))
    hi = lax.ppermute(minus, AXES, hop(-1, 0))
    (part,) = call(functools.partial(lower_kernel, 0), [(8 * ROWS, 128)], got, lo, ym, xm)
    own, plus, minus = call(
        first_kernel, [(8, ROWS, 128), (6, ROWS, 128), (6, ROWS, 128)], part, hi, ym, xu
    )
    lo = lax.ppermute(plus, AXES, hop(1, 1))
    hi = lax.ppermute(minus, AXES, hop(-1, 1))
    (part,) = call(functools.partial(lower_kernel, 1), [(8 * ROWS, 128)], own, lo, ym, xm)
    (sent,) = call(second_kernel, [(8, ROWS, 128)], part, hi, ym, xu)
    got = lax.all_to_all(sent, AXES, split_axis=0, concat_axis=0, tiled=True, axis_index_groups=eights)
    (out,) = call(last_kernel, [(768, 512)], got, scaling.reshape(768, 512), plain=True)
    return out.reshape(16, 48, 512)


def solution(mesh):
    eights, hop = links(mesh)
    in_specs = (P("grp", "blk", None), P("blk", None), P(), P(), P("grp", "blk", None))
    return jax.shard_map(
        functools.partial(on_device, eights, hop),
        mesh=mesh,
        in_specs=in_specs,
        out_specs=P("grp", "blk", None),
        check_vma=False,
    )
```

```python
import functools

import jax
import jax.numpy as jnp
from jax import lax
from jax.experimental import pallas as pl
from jax.experimental.pallas import tpu as pltpu
from jax.sharding import PartitionSpec as P

AXES = ("blk", "grp")
ROWS = 384
EXTRA = 24
INTERPRET = False
Y_UNROLL = 12
X_UNROLL = 4
Z_PAIRS = 2
Z_WAIT = 4
VMEM_LIMIT = 24 * 2**20


def split(v):
    hi = v.astype(jnp.bfloat16)
    return hi, (v - hi.astype(jnp.float32)).astype(jnp.bfloat16)


def dot3(a, b, dims):
    (ah, al), (bh, bl) = a, b
    mul = lambda p, q: lax.dot_general(p, q, (dims, ((), ())), preferred_element_type=jnp.float32)
    return mul(ah, bh) + (mul(ah, bl) + mul(al, bh))


def stack(m):
    return jnp.concatenate(split(m), axis=0)


def factor_dot(m, cols):
    n = m.shape[0] // 2
    ch, cl = split(cols)
    mul = lambda p, q: lax.dot_general(p, q, (((1,), (0,)), ((), ())), preferred_element_type=jnp.float32)
    both = mul(m, ch)
    return both[:n] + (both[n:] + mul(m[:n], cl))


def halves(a, b, low):
    return jnp.where(low, a, pltpu.roll(b, 64, 1)), jnp.where(low, pltpu.roll(a, 64, 1), b)


def core_of():
    return lax.rem(lax.axis_index("grp"), 2)


def low_lanes(rows):
    return lax.broadcasted_iota(jnp.int32, (rows, 128), 1) < 64


class Pair:
    def __init__(self, *copies):
        self.copies = copies

    def start(self):
        for c in self.copies:
            c.start()

    def wait(self):
        for c in self.copies:
            c.wait()


def beside(rows, t, low):
    tile = lambda k: rows[:, 128 * (k % 4) : 128 * (k % 4) + 128]
    return jnp.concatenate([tile(t), jnp.where(low, tile(t + 1), tile(t - 1))], axis=1)


def depth_kernel(field_hbm, z_hbm, panel_hbm, out_ref, field_ref, z_ref, w_ref, panel_ref, sems):
    panel_copy = pltpu.make_async_copy(panel_hbm, panel_ref, sems.at[18])
    field_copies, z_copies = [], []
    for u in range(2):
        at = pl.ds(256 * u, 256)
        z_copies.append(pltpu.make_async_copy(z_hbm.at[at, :], z_ref.at[at, :], sems.at[16 + u]))
    for y in range(8):
        for i in range(2):
            at = pl.ds(48 * (8 * i + y), 48)
            field_copies.append(pltpu.make_async_copy(field_hbm.at[at, :], field_ref.at[at, :], sems.at[2 * y + i]))
    field_copies = [Pair(*field_copies[2 * y : 2 * y + 2]) for y in range(8)]
    for c in z_copies + field_copies + [panel_copy]:
        c.start()

    for c in z_copies:
        c.wait()
    for t in range(4):
        both = split(beside(z_ref[pl.ds(128 * t, 128), :], t, low_lanes(128)))
        w_ref[t] = jnp.concatenate(both, axis=0)
    low = low_lanes(48)
    for m in range(8 // Z_PAIRS):
        ys = [Z_PAIRS * m + i for i in range(Z_PAIRS)]
        if (Z_PAIRS * m) % Z_WAIT == 0:
            for c in field_copies[Z_PAIRS * m : Z_PAIRS * m + Z_WAIT]:
                c.wait()
        ys = ys + [8 + y for y in ys]
        n = 48 * len(ys)
        rows = jnp.concatenate([field_ref[pl.ds(48 * y, 48), :] for y in ys], axis=0)
        for t in range(4):
            r = lax.dot_general(
                jnp.concatenate(split(beside(rows, t, low_lanes(n))), axis=0), w_ref[t],
                (((1,), (1,)), ((), ())), preferred_element_type=jnp.float32,
            )
            tile = r[:n, :128] + (r[:n, 128:] + r[n:, :128])
            d = 2 * t
            for i, y in enumerate(ys):
                part = tile[48 * i : 48 * i + 48]
                e = jnp.where(low_lanes(24), part[:24], pltpu.roll(part[24:], 64, 1))
                out_ref[d, pl.ds(y, 24, stride=16), :] = e
            for i in range(Z_PAIRS):
                a = tile[48 * i : 48 * i + 48]
                b = tile[48 * (Z_PAIRS + i) : 48 * (Z_PAIRS + i) + 48]
                out_ref[d + 1, pl.ds(48 * ys[i], 48), :] = jnp.where(low, pltpu.roll(a, 64, 1), b)

    panel_copy.wait()
    share = lax.rem(lax.axis_index("grp"), 4)
    for s in range(4):
        @pl.when(share == s)
        def _():
            rows = panel_ref[pl.ds(12 * s, 12), :]
            for d in range(8):
                out_ref[d, pl.ds(ROWS, 12), :] = rows[:, :128]
                out_ref[d, pl.ds(ROWS + 12, 12), pl.ds(0, 16)] = rows[:, 128:]


def loop(count, unroll, body):
    def step(i, carry):
        for k in range(unroll):
            body(unroll * i + k)
        return carry

    lax.fori_loop(0, count // unroll, step, 0)


def pair_of(body):
    return [body(0), body(1)]


def y_rows(x):
    return pl.ds(pl.multiple_of(16 * x, 16), 16)


def x_rows(y):
    return pl.ds(pl.multiple_of(48 * y, 16), 48)


def keep(part, at, n, r):
    for j in range(2):
        part[pl.ds(pl.multiple_of(n * (at + j), 32), n), :] = r[:, 128 * j : 128 * j + 128]


def part_rows(part, at, n):
    return part[pl.ds(pl.multiple_of(n * at, 32), n), :]


def lower_kernel(y_core, own, lo, ym, xm, part):
    core = core_of()

    @pl.when(core == y_core)
    def _():
        ys = stack(ym[:, :112])
        for xh in range(2):
            def body(i):
                def column(j):
                    at = y_rows(2 * i + j)
                    return jnp.concatenate(
                        [lo[3 * xh + s, at, :] for s in range(3)] + [own[4 * xh + s, at, :] for s in range(4)], axis=0
                    )

                keep(part, 24 * xh + 2 * i, 64, factor_dot(ys, jnp.concatenate(pair_of(column), axis=1)))

            loop(12, Y_UNROLL, body)

    @pl.when(core != y_core)
    def _():
        xs = stack(xm[:, :144])
        for s in range(4):
            def body(i):
                def column(j):
                    at = x_rows(2 * i + j)
                    return jnp.concatenate([lo[s, at, :], own[s, at, :], own[4 + s, at, :]], axis=0)

                keep(part, 8 * s + 2 * i, 96, factor_dot(xs, jnp.concatenate(pair_of(column), axis=1)))

            loop(4, X_UNROLL, body)


def y_finish(part, hi, ym, emit):
    ys = stack(ym[:, 128:176])
    for xh in range(2):
        def body(i):
            def column(j):
                return jnp.concatenate([hi[3 * xh + s, y_rows(2 * i + j), :] for s in range(3)], axis=0)

            r = factor_dot(ys, jnp.concatenate(pair_of(column), axis=1))
            for j in range(2):
                x = 2 * i + j
                emit(xh, x, part_rows(part, 24 * xh + x, 64) + r[:, 128 * j : 128 * j + 128])

        loop(12, Y_UNROLL, body)


def x_finish(part, hi, xu, emit):
    xs = stack(xu[:, :48])
    for s in range(4):
        def body(i):
            r = factor_dot(xs, jnp.concatenate(pair_of(lambda j: hi[s, x_rows(2 * i + j), :]), axis=1))
            for j in range(2):
                y = 2 * i + j
                p = part_rows(part, 8 * s + y, 96)
                emit(s, y, (p[:48], p[48:] + r[:, 128 * j : 128 * j + 128]))

        loop(4, X_UNROLL, body)


def pick_kernel(own, y_ref, plus, minus, ym, xm, xu):
    core = core_of()
    slab = lax.div(lax.axis_index("grp"), 4)
    ny = y_ref.shape[0]
    @pl.when(core == 0)
    def _():
        for i, (p, m) in enumerate(((1, 0), (2, 1), (3, 2), (5, 4), (6, 5), (7, 6))):
            plus[i] = own[p, pl.ds(0, ROWS), :]
            minus[i] = own[m, pl.ds(0, ROWS), :]

    @pl.when(core == 1)
    def _():
        for s in range(4):
            plus[s] = own[4 + s, pl.ds(0, ROWS), :]
            minus[s] = own[s, pl.ds(0, ROWS), :]

    few = lax.broadcasted_iota(jnp.int32, (12, 128), 1) < 16
    for xh in range(2):
        for s in range(4):
            p = own[4 * xh + s, pl.ds(ROWS, 12), :]
            q = jnp.where(few, own[4 * xh + s, pl.ds(ROWS + 12, 12), :], 0.0)
            w = jnp.concatenate([p, q], axis=1)
            xm[pl.ds(48 * xh + 12 * s, 12), :] = pltpu.roll(w, 48, 1) if xh else w
            if xh:
                xu[pl.ds(12 * s, 12), :] = pltpu.roll(w, 160, 1)[:, :128]
    rows = y_ref[pl.ds(pl.multiple_of(64 * slab, 64), 64), :]
    for i, first in enumerate((-48, 64)):
        shift = lax.rem(2 * ny - first - 64 * slab, ny)
        ym[:, pl.ds(128 * i, 128)] = pltpu.roll(rows, shift, 1)[:, :128]


def first_kernel(part, hi, ym, xu, out, plus, minus):
    core = core_of()

    @pl.when(core == 0)
    def _():
        def emit(xh, xx, r):
            for s in range(4):
                w = halves(r[16 * s : 16 * s + 8], r[16 * s + 8 : 16 * s + 16], low_lanes(8))
                for h in range(2):
                    out[4 * xh + s, pl.ds(24 * h + xx, 8, stride=48), :] = w[h]

        y_finish(part, hi, ym, emit)
        for s in range(4):
            plus[s] = out[4 + s]
            minus[s] = out[s]

    @pl.when(core == 1)
    def _():
        def emit(s, yy, r):
            for xh in range(2):
                q = halves(r[xh][:24], r[xh][24:], low_lanes(24))
                for yh in range(2):
                    out[4 * xh + s, pl.ds(8 * yh + yy, 24, stride=16), :] = q[yh]

        x_finish(part, hi, xu, emit)
        for xh in range(2):
            for s in range(3):
                plus[3 * xh + s] = out[4 * xh + s + 1]
                minus[3 * xh + s] = out[4 * xh + s]


def second_kernel(part, hi, ym, xu, out):
    core = core_of()

    @pl.when(core == 0)
    def _():
        def emit(s, yy, r):
            for xh in range(2):
                out[4 * xh + s, x_rows(yy), :] = r[xh]

        x_finish(part, hi, xu, emit)

    @pl.when(core == 1)
    def _():
        def emit(xh, xx, r):
            for s in range(4):
                out[4 * xh + s, y_rows(xx), :] = r[16 * s : 16 * s + 16]

        y_finish(part, hi, ym, emit)


def last_kernel(got, scale_ref, out_ref):
    low = low_lanes(24)
    for t in range(4):
        lanes = pl.ds(128 * t, 128)
        for yy in range(8):
            a = got[2 * t, pl.ds(48 * yy, 48), :]
            for yh in range(2):
                y = 8 * yh + yy
                c = got[2 * t + 1, pl.ds(y, 24, stride=16), :]
                c2 = pltpu.roll(c, 64, 1)
                a2 = pltpu.roll(a, 64, 1) if yh else a
                for h in range(2):
                    at = pl.ds(48 * y + 24 * h, 24)
                    r = jnp.where(low, a2[24 * h : 24 * h + 24], c if h else c2)
                    out_ref[at, lanes] = r * scale_ref[at, lanes]


def call(kernel, shapes, *args, hbm=(), plain=False, scratch=()):
    vmem = pl.BlockSpec(memory_space=pltpu.VMEM)
    outs = [jax.ShapeDtypeStruct(s, jnp.float32) for s in shapes]
    if not INTERPRET:
        args = [pltpu.with_memory_space_constraint(a, pltpu.HBM if i in hbm else pltpu.VMEM) for i, a in enumerate(args)]
        if not plain:
            outs = [pltpu.VMEM(s, jnp.float32) for s in shapes]
    return pl.pallas_call(
        kernel,
        out_shape=outs,
        in_specs=[pl.BlockSpec(memory_space=pltpu.HBM) if i in hbm else vmem for i in range(len(args))],
        out_specs=[vmem for _ in shapes],
        scratch_shapes=list(scratch),
        compiler_params=pltpu.CompilerParams(vmem_limit_bytes=VMEM_LIMIT),
        interpret=INTERPRET,
    )(*args)


def links(mesh):
    n_blk, n_grp = mesh.shape["blk"], mesh.shape["grp"]
    n_y, n_z = n_blk // 2, n_grp // 4

    def place(y, xh, z, r):
        return ((y % n_y) * 2 + xh) * n_grp + (z % n_z) * 4 + r

    everyone = [(y, xh, z, r) for y in range(n_y) for xh in range(2) for z in range(n_z) for r in range(4)]

    def hop(step, along_z):
        pairs = []
        for y, xh, z, r in everyone:
            if r % 2 == along_z:
                to = place(y, xh, z + step, r)
            else:
                to = place(y + step, xh, z, r)
            pairs.append((place(y, xh, z, r), to))
        return pairs

    eights = [[place(y, xh, z, r) for xh in range(2) for r in range(4)] for y in range(n_y) for z in range(n_z)]
    return eights, hop


def on_device(eights, hop, field, x_panel, y_factor, z_factor, scaling):
    (sent,) = call(
        depth_kernel, [(8, ROWS + EXTRA, 128)], field.reshape(768, 512), z_factor, x_panel,
        hbm=(0, 1, 2),
        scratch=[
            pltpu.VMEM((768, 512), jnp.float32),
            pltpu.VMEM((512, 512), jnp.float32),
            pltpu.VMEM((4, 256, 256), jnp.bfloat16),
            pltpu.VMEM((48, 144), jnp.float32),
            pltpu.SemaphoreType.DMA((19,)),
        ],
    )
    got = lax.all_to_all(sent, AXES, split_axis=0, concat_axis=0, tiled=True, axis_index_groups=eights)

    plus, minus, ym, xm, xu = call(
        pick_kernel, [(6, ROWS, 128), (6, ROWS, 128), (64, 256), (96, 256), (48, 128)], got, y_factor
    )
    lo = lax.ppermute(plus, AXES, hop(1, 0))
    hi = lax.ppermute(minus, AXES, hop(-1, 0))
    (part,) = call(functools.partial(lower_kernel, 0), [(8 * ROWS, 128)], got, lo, ym, xm)
    own, plus, minus = call(
        first_kernel, [(8, ROWS, 128), (6, ROWS, 128), (6, ROWS, 128)], part, hi, ym, xu
    )
    lo = lax.ppermute(plus, AXES, hop(1, 1))
    hi = lax.ppermute(minus, AXES, hop(-1, 1))
    (part,) = call(functools.partial(lower_kernel, 1), [(8 * ROWS, 128)], own, lo, ym, xm)
    (sent,) = call(second_kernel, [(8, ROWS, 128)], part, hi, ym, xu)
    got = lax.all_to_all(sent, AXES, split_axis=0, concat_axis=0, tiled=True, axis_index_groups=eights)
    (out,) = call(last_kernel, [(768, 512)], got, scaling.reshape(768, 512), plain=True)
    return out.reshape(16, 48, 512)


def solution(mesh):
    eights, hop = links(mesh)
    in_specs = (P("grp", "blk", None), P("blk", None), P(), P(), P("grp", "blk", None))
    return jax.shard_map(
        functools.partial(on_device, eights, hop),
        mesh=mesh,
        in_specs=in_specs,
        out_specs=P("grp", "blk", None),
        check_vma=False,
    )
```

```python
import functools

import jax
import jax.numpy as jnp
from jax import lax
from jax.experimental import pallas as pl
from jax.experimental.pallas import tpu as pltpu
from jax.sharding import PartitionSpec as P

AXES = ("blk", "grp")
ROWS = 384
EXTRA = 24
INTERPRET = False
Y_UNROLL = 12
X_UNROLL = 4
Z_PAIRS = 2
Z_WAIT = 4
VMEM_LIMIT = 24 * 2**20


def split(v):
    hi = v.astype(jnp.bfloat16)
    return hi, (v - hi.astype(jnp.float32)).astype(jnp.bfloat16)


def dot3(a, b, dims):
    (ah, al), (bh, bl) = a, b
    mul = lambda p, q: lax.dot_general(p, q, (dims, ((), ())), preferred_element_type=jnp.float32)
    return mul(ah, bh) + (mul(ah, bl) + mul(al, bh))


def stack(m):
    return jnp.concatenate(split(m), axis=0)


def factor_dot(m, cols):
    n = m.shape[0] // 2
    ch, cl = split(cols)
    mul = lambda p, q: lax.dot_general(p, q, (((1,), (0,)), ((), ())), preferred_element_type=jnp.float32)
    both = mul(m, ch)
    return both[:n] + (both[n:] + mul(m[:n], cl))


def halves(a, b, low):
    return jnp.where(low, a, pltpu.roll(b, 64, 1)), jnp.where(low, pltpu.roll(a, 64, 1), b)


def core_of():
    return lax.rem(lax.axis_index("grp"), 2)


def parities():
    along_y = lax.rem(lax.div(lax.axis_index("blk"), 2), 2)
    return along_y, lax.rem(lax.div(lax.axis_index("grp"), 4), 2)


def put(first, second, parity, up, down):
    for p, (u, d) in enumerate(((first, second), (second, first))):
        @pl.when(parity == p)
        def _():
            for i in range(len(up)):
                u[i] = up[i]()
                d[i] = down[i]()


def low_lanes(rows):
    return lax.broadcasted_iota(jnp.int32, (rows, 128), 1) < 64


class Pair:
    def __init__(self, *copies):
        self.copies = copies

    def start(self):
        for c in self.copies:
            c.start()

    def wait(self):
        for c in self.copies:
            c.wait()


def beside(rows, t, low):
    tile = lambda k: rows[:, 128 * (k % 4) : 128 * (k % 4) + 128]
    return jnp.concatenate([tile(t), jnp.where(low, tile(t + 1), tile(t - 1))], axis=1)


def depth_kernel(field_hbm, z_hbm, panel_hbm, out_ref, field_ref, z_ref, w_ref, panel_ref, sems):
    panel_copy = pltpu.make_async_copy(panel_hbm, panel_ref, sems.at[18])
    field_copies, z_copies = [], []
    for u in range(2):
        at = pl.ds(256 * u, 256)
        z_copies.append(pltpu.make_async_copy(z_hbm.at[at, :], z_ref.at[at, :], sems.at[16 + u]))
    for y in range(8):
        for i in range(2):
            at = pl.ds(48 * (8 * i + y), 48)
            field_copies.append(pltpu.make_async_copy(field_hbm.at[at, :], field_ref.at[at, :], sems.at[2 * y + i]))
    field_copies = [Pair(*field_copies[2 * y : 2 * y + 2]) for y in range(8)]
    for c in z_copies + field_copies + [panel_copy]:
        c.start()

    for c in z_copies:
        c.wait()
    for t in range(4):
        both = split(beside(z_ref[pl.ds(128 * t, 128), :], t, low_lanes(128)))
        w_ref[t] = jnp.concatenate(both, axis=0)
    low = low_lanes(48)
    for m in range(8 // Z_PAIRS):
        ys = [Z_PAIRS * m + i for i in range(Z_PAIRS)]
        if (Z_PAIRS * m) % Z_WAIT == 0:
            for c in field_copies[Z_PAIRS * m : Z_PAIRS * m + Z_WAIT]:
                c.wait()
        ys = ys + [8 + y for y in ys]
        n = 48 * len(ys)
        rows = jnp.concatenate([field_ref[pl.ds(48 * y, 48), :] for y in ys], axis=0)
        for t in range(4):
            r = lax.dot_general(
                jnp.concatenate(split(beside(rows, t, low_lanes(n))), axis=0), w_ref[t],
                (((1,), (1,)), ((), ())), preferred_element_type=jnp.float32,
            )
            tile = r[:n, :128] + (r[:n, 128:] + r[n:, :128])
            d = 2 * t
            for i, y in enumerate(ys):
                part = tile[48 * i : 48 * i + 48]
                e = jnp.where(low_lanes(24), part[:24], pltpu.roll(part[24:], 64, 1))
                out_ref[d, pl.ds(y, 24, stride=16), :] = e
            for i in range(Z_PAIRS):
                a = tile[48 * i : 48 * i + 48]
                b = tile[48 * (Z_PAIRS + i) : 48 * (Z_PAIRS + i) + 48]
                out_ref[d + 1, pl.ds(48 * ys[i], 48), :] = jnp.where(low, pltpu.roll(a, 64, 1), b)

    panel_copy.wait()
    share = lax.rem(lax.axis_index("grp"), 4)
    for s in range(4):
        @pl.when(share == s)
        def _():
            rows = panel_ref[pl.ds(12 * s, 12), :]
            for d in range(8):
                out_ref[d, pl.ds(ROWS, 12), :] = rows[:, :128]
                out_ref[d, pl.ds(ROWS + 12, 12), pl.ds(0, 16)] = rows[:, 128:]


def loop(count, unroll, body):
    def step(i, carry):
        for k in range(unroll):
            body(unroll * i + k)
        return carry

    lax.fori_loop(0, count // unroll, step, 0)


def pair_of(body):
    return [body(0), body(1)]


def y_rows(x):
    return pl.ds(pl.multiple_of(16 * x, 16), 16)


def x_rows(y):
    return pl.ds(pl.multiple_of(48 * y, 16), 48)


def keep(part, at, n, r):
    for j in range(2):
        part[pl.ds(pl.multiple_of(n * (at + j), 32), n), :] = r[:, 128 * j : 128 * j + 128]


def part_rows(part, at, n):
    return part[pl.ds(pl.multiple_of(n * at, 32), n), :]


def lower_kernel(y_core, own, near, ym, xm, part):
    core = core_of()

    @pl.when(core == y_core)
    def _():
        ys = stack(ym[:, :112])
        for xh in range(2):
            def body(i):
                def column(j):
                    at = y_rows(2 * i + j)
                    return jnp.concatenate(
                        [near[3 * xh + s, at, :] for s in range(3)] + [own[4 * xh + s, at, :] for s in range(4)], axis=0
                    )

                keep(part, 24 * xh + 2 * i, 64, factor_dot(ys, jnp.concatenate(pair_of(column), axis=1)))

            loop(12, Y_UNROLL, body)

    @pl.when(core != y_core)
    def _():
        xs = stack(xm[:, :144])
        for s in range(4):
            def body(i):
                def column(j):
                    at = x_rows(2 * i + j)
                    return jnp.concatenate([near[s, at, :], own[s, at, :], own[4 + s, at, :]], axis=0)

                keep(part, 8 * s + 2 * i, 96, factor_dot(xs, jnp.concatenate(pair_of(column), axis=1)))

            loop(4, X_UNROLL, body)


def y_finish(part, hi, ym, emit):
    ys = stack(ym[:, 128:176])
    for xh in range(2):
        def body(i):
            def column(j):
                return jnp.concatenate([hi[3 * xh + s, y_rows(2 * i + j), :] for s in range(3)], axis=0)

            r = factor_dot(ys, jnp.concatenate(pair_of(column), axis=1))
            for j in range(2):
                x = 2 * i + j
                emit(xh, x, part_rows(part, 24 * xh + x, 64) + r[:, 128 * j : 128 * j + 128])

        loop(12, Y_UNROLL, body)


def x_finish(part, hi, xu, emit):
    xs = stack(xu[:, :48])
    for s in range(4):
        def body(i):
            r = factor_dot(xs, jnp.concatenate(pair_of(lambda j: hi[s, x_rows(2 * i + j), :]), axis=1))
            for j in range(2):
                y = 2 * i + j
                p = part_rows(part, 8 * s + y, 96)
                p = p + r[:, 128 * j : 128 * j + 128]
                emit(s, y, (p[:48], p[48:]))

        loop(4, X_UNROLL, body)


def pick_kernel(own, y_ref, early, late_send, ym, xm, xu):
    core = core_of()
    slab = lax.div(lax.axis_index("grp"), 4)
    ny = y_ref.shape[0]
    along_y, along_z = parities()
    block = lambda k: lambda: own[k, pl.ds(0, ROWS), :]

    @pl.when(core == 0)
    def _():
        put(early, late_send, along_z, [block(k) for k in (1, 2, 3, 5, 6, 7)], [block(k) for k in (0, 1, 2, 4, 5, 6)])

    @pl.when(core == 1)
    def _():
        put(early, late_send, along_y, [block(k) for k in (4, 5, 6, 7)], [block(k) for k in (0, 1, 2, 3)])

    head = lax.broadcasted_iota(jnp.int32, (12, 256), 1) < 48
    few = lax.broadcasted_iota(jnp.int32, (12, 128), 1) < 16
    for xh in range(2):
        for s in range(4):
            p = own[4 * xh + s, pl.ds(ROWS, 12), :]
            q = jnp.where(few, own[4 * xh + s, pl.ds(ROWS + 12, 12), :], 0.0)
            w = jnp.concatenate([p, q], axis=1)
            at = pl.ds(48 * xh + 12 * s, 12)
            here = w if xh == 0 else pltpu.roll(w, 48, 1)
            other = jnp.zeros_like(w) if xh == 0 else pltpu.roll(w, 160, 1)
            xm[at, :] = jnp.where(jnp.logical_and(head, along_y == 0), other, here)
            late = (w[:, :128], jnp.zeros((12, 128), jnp.float32))
            if xh:
                late = (late[1], other[:, :128])
            xu[at, :] = jnp.where(along_y == 0, late[0], late[1])
    rows = y_ref[pl.ds(pl.multiple_of(64 * slab, 64), 64), :]
    down, up = [pltpu.roll(rows, lax.rem(2 * ny - k - 64 * slab, ny), 1)[:, :128] for k in (-48, 64)]
    head = lax.broadcasted_iota(jnp.int32, (64, 128), 1) < 48
    ym[:, pl.ds(0, 128)] = jnp.where(jnp.logical_and(head, along_z == 0), up, down)
    ym[:, pl.ds(128, 128)] = jnp.where(along_z == 0, down, up)


def first_kernel(part, hi, ym, xu, out, early, late_send):
    core = core_of()
    along_y, along_z = parities()
    block = lambda k: lambda: out[k]

    @pl.when(core == 0)
    def _():
        def emit(xh, xx, r):
            for s in range(4):
                w = halves(r[16 * s : 16 * s + 8], r[16 * s + 8 : 16 * s + 16], low_lanes(8))
                for h in range(2):
                    out[4 * xh + s, pl.ds(24 * h + xx, 8, stride=48), :] = w[h]

        y_finish(part, hi, ym, emit)
        put(early, late_send, along_y, [block(k) for k in (4, 5, 6, 7)], [block(k) for k in (0, 1, 2, 3)])

    @pl.when(core == 1)
    def _():
        def emit(s, yy, r):
            for xh in range(2):
                q = halves(r[xh][:24], r[xh][24:], low_lanes(24))
                for yh in range(2):
                    out[4 * xh + s, pl.ds(8 * yh + yy, 24, stride=16), :] = q[yh]

        x_finish(part, hi, xu, emit)
        put(early, late_send, along_z, [block(k) for k in (1, 2, 3, 5, 6, 7)], [block(k) for k in (0, 1, 2, 4, 5, 6)])


def second_kernel(part, hi, ym, xu, out):
    core = core_of()

    @pl.when(core == 0)
    def _():
        def emit(s, yy, r):
            for xh in range(2):
                out[4 * xh + s, x_rows(yy), :] = r[xh]

        x_finish(part, hi, xu, emit)

    @pl.when(core == 1)
    def _():
        def emit(xh, xx, r):
            for s in range(4):
                out[4 * xh + s, y_rows(xx), :] = r[16 * s : 16 * s + 16]

        y_finish(part, hi, ym, emit)


def last_kernel(got, scale_ref, out_ref):
    low = low_lanes(24)
    for t in range(4):
        lanes = pl.ds(128 * t, 128)
        for yy in range(8):
            a = got[2 * t, pl.ds(48 * yy, 48), :]
            for yh in range(2):
                y = 8 * yh + yy
                c = got[2 * t + 1, pl.ds(y, 24, stride=16), :]
                c2 = pltpu.roll(c, 64, 1)
                a2 = pltpu.roll(a, 64, 1) if yh else a
                for h in range(2):
                    at = pl.ds(48 * y + 24 * h, 24)
                    r = jnp.where(low, a2[24 * h : 24 * h + 24], c if h else c2)
                    out_ref[at, lanes] = r * scale_ref[at, lanes]


def call(kernel, shapes, *args, hbm=(), plain=False, scratch=()):
    vmem = pl.BlockSpec(memory_space=pltpu.VMEM)
    outs = [jax.ShapeDtypeStruct(s, jnp.float32) for s in shapes]
    if not INTERPRET:
        args = [pltpu.with_memory_space_constraint(a, pltpu.HBM if i in hbm else pltpu.VMEM) for i, a in enumerate(args)]
        if not plain:
            outs = [pltpu.VMEM(s, jnp.float32) for s in shapes]
    return pl.pallas_call(
        kernel,
        out_shape=outs,
        in_specs=[pl.BlockSpec(memory_space=pltpu.HBM) if i in hbm else vmem for i in range(len(args))],
        out_specs=[vmem for _ in shapes],
        scratch_shapes=list(scratch),
        compiler_params=pltpu.CompilerParams(vmem_limit_bytes=VMEM_LIMIT),
        interpret=INTERPRET,
    )(*args)


def links(mesh):
    n_blk, n_grp = mesh.shape["blk"], mesh.shape["grp"]
    n_y, n_z = n_blk // 2, n_grp // 4

    def place(y, xh, z, r):
        return ((y % n_y) * 2 + xh) * n_grp + (z % n_z) * 4 + r

    everyone = [(y, xh, z, r) for y in range(n_y) for xh in range(2) for z in range(n_z) for r in range(4)]

    def hop(turn, along_z):
        pairs = []
        for y, xh, z, r in everyone:
            if r % 2 == along_z:
                to = place(y, xh, z + (1 if z % 2 == turn else -1), r)
            else:
                to = place(y + (1 if y % 2 == turn else -1), xh, z, r)
            pairs.append((place(y, xh, z, r), to))
        return pairs

    eights = [[place(y, xh, z, r) for xh in range(2) for r in range(4)] for y in range(n_y) for z in range(n_z)]
    return eights, hop


def on_device(eights, hop, field, x_panel, y_factor, z_factor, scaling):
    (sent,) = call(
        depth_kernel, [(8, ROWS + EXTRA, 128)], field.reshape(768, 512), z_factor, x_panel,
        hbm=(0, 1, 2),
        scratch=[
            pltpu.VMEM((768, 512), jnp.float32),
            pltpu.VMEM((512, 512), jnp.float32),
            pltpu.VMEM((4, 256, 256), jnp.bfloat16),
            pltpu.VMEM((48, 144), jnp.float32),
            pltpu.SemaphoreType.DMA((19,)),
        ],
    )
    got = lax.all_to_all(sent, AXES, split_axis=0, concat_axis=0, tiled=True, axis_index_groups=eights)

    early, late_send, ym, xm, xu = call(
        pick_kernel, [(6, ROWS, 128), (6, ROWS, 128), (64, 256), (96, 256), (96, 128)], got, y_factor
    )
    near = lax.ppermute(early, AXES, hop(0, 0))
    hi = lax.ppermute(late_send, AXES, hop(1, 0))
    (part,) = call(functools.partial(lower_kernel, 0), [(8 * ROWS, 128)], got, near, ym, xm)
    own, early, late_send = call(
        first_kernel, [(8, ROWS, 128), (6, ROWS, 128), (6, ROWS, 128)], part, hi, ym, xu
    )
    near = lax.ppermute(early, AXES, hop(0, 1))
    hi = lax.ppermute(late_send, AXES, hop(1, 1))
    (part,) = call(functools.partial(lower_kernel, 1), [(8 * ROWS, 128)], own, near, ym, xm)
    (sent,) = call(second_kernel, [(8, ROWS, 128)], part, hi, ym, xu)
    got = lax.all_to_all(sent, AXES, split_axis=0, concat_axis=0, tiled=True, axis_index_groups=eights)
    (out,) = call(last_kernel, [(768, 512)], got, scaling.reshape(768, 512), plain=True)
    return out.reshape(16, 48, 512)


def solution(mesh):
    eights, hop = links(mesh)
    in_specs = (P("grp", "blk", None), P("blk", None), P(), P(), P("grp", "blk", None))
    return jax.shard_map(
        functools.partial(on_device, eights, hop),
        mesh=mesh,
        in_specs=in_specs,
        out_specs=P("grp", "blk", None),
        check_vma=False,
    )
```
